32 devices in a mesh: rep: 4 (over x, core), shard: 8 (over z, y).
Axes of the slice: x: 2, y: 2, z: 4, core: 2. Of those that a mesh axis runs over, the one named last changes fastest.
Arguments:
- x_in: bfloat16 [8192, 768], P(('rep', 'shard')), may hold values from -6 to 6
- cotangent: bfloat16 [8192, 768], P(('rep', 'shard')), may hold values from -6 to 6
- counts: int32 [32], P(('rep', 'shard')), may hold values from 64 to 256, as said below
- seg_ids: int32 [8192], P(('rep', 'shard')), may hold values from 0 to 8, as said below
- w_in: float32 [768, 3352], P('shard'), may hold values from -0.21875 to 0.21875
- w_out: float32 [1536, 768], P('shard'), may hold values from -0.15625 to 0.15625
- conv_p: float32 [5, 1792], P(None, 'shard'), may hold values from -3 to 3
- norm_gain: float32 [768], P('shard'), may hold values from 0.5 to 1.5
- gate_gain: float32 [1536], P('shard'), may hold values from 0.5 to 1.5
- head_p: float32 [3, 24], replicated, may hold values from -6 to 2.5
- mom_in: float32 [2, 768, 3352], P(None, 'shard'), may hold values from -13.57645 to 13.57645, as said below
- mom_out: float32 [2, 1536, 768], P(None, 'shard'), may hold values from -13.57645 to 13.57645, as said below
- mom_conv: float32 [2, 5, 1792], P(None, None, 'shard'), may hold values from -13.57645 to 13.57645, as said below
- mom_norm: float32 [2, 768], P(None, 'shard'), may hold values from -13.57645 to 13.57645, as said below
- mom_gate: float32 [2, 1536], P(None, 'shard'), may hold values from -13.57645 to 13.57645, as said below
- mom_head: float32 [2, 3, 24], replicated, may hold values from -13.57645 to 13.57645, as said below
Outputs:
- block_out: bfloat16 [8192, 768], P(('rep', 'shard'))
- input_grad: float32 [8192, 768], P(('rep', 'shard'))
- grad_in: float32 [768, 3352], P('shard')
- grad_out: float32 [1536, 768], P('shard')
- grad_conv: float32 [5, 1792], P(None, 'shard')
- grad_norm: float32 [768], P('shard')
- grad_gate: float32 [1536], P('shard')
- grad_head: float32 [3, 24], replicated
- new_in: float32 [768, 3352], P('shard')
- new_out: float32 [1536, 768], P('shard')
- new_conv: float32 [5, 1792], P(None, 'shard')
- new_norm: float32 [768], P('shard')
- new_gate: float32 [1536], P('shard')
- new_head: float32 [3, 24], replicated
- new_mom_in: float32 [2, 768, 3352], P(None, 'shard')
- new_mom_out: float32 [2, 1536, 768], P(None, 'shard')
- new_mom_conv: float32 [2, 5, 1792], P(None, None, 'shard')
- new_mom_norm: float32 [2, 768], P(None, 'shard')
- new_mom_gate: float32 [2, 1536], P(None, 'shard')
- new_mom_head: float32 [2, 3, 24], replicated
The draws below stay inside these ranges and needn't reach their ends.
Inputs may be any that keep to these rules, and one draw needn't show every extreme that they name: `counts`: each device's live tokens fill its first slots; one device is full and one holds 64. `seg_ids`: within each device's 256 slots the ids start at 0 and rise by 0 or 1 from slot to slot; a new id may start only at a multiple of 32 or at the device's first slot after its live tokens, where one always starts; some device reaches the largest id. `mom_in`: row 1 is positive. `mom_out`: row 1 is positive. `mom_conv`: row 1 is positive. `mom_norm`: row 1 is positive. `mom_gate`: row 1 is positive. `mom_head`: row 1 is positive.
All inputs are finite; a program needn't handle non-finite values.
Results may differ from the reference program's by a relative error of at most 0.012.
The reference program's roundings to bfloat16 on the way count: a program that leaves them out, or rounds other values in their place, can miss the bound.
Values may be sent and summed in bfloat16 or wider, within the bound.
A program may use at most 128 MiB of HBM per device.

```python
import math
import jax
import jax.numpy as jnp
from jax import lax

D = 768
HEADDIM = 64
STATE = 128
KERNEL = 4
SPAN = 256
STEP = 3
TOK_DEV = 256
INNER = 1536
HEADS = 24
CONVD = 1792
PROJ = 3352
TOKENS = 8192
DEVICES = 32


def layout(key):
    base = jax.random.fold_in(key, 101)
    count_key, cut_key = jax.random.split(base)
    device_ids = jnp.arange(DEVICES)
    drawn = jax.random.randint(count_key, (DEVICES,), TOK_DEV // 4, TOK_DEV + 1)
    odd_count = TOK_DEV // 2 + TOK_DEV // 16
    drawn = jnp.where(device_ids == 0, TOK_DEV, jnp.where(device_ids == 1, TOK_DEV // 4, jnp.where(device_ids == 2, odd_count, drawn))).astype(jnp.int32)
    slots = jnp.arange(TOK_DEV)[None, :]
    allowed = slots % (TOK_DEV // 8) == 0
    coin = jax.random.randint(cut_key, (DEVICES, TOK_DEV), 0, 2) == 0
    forced = (device_ids == 0) | (device_ids == 2)
    cuts = allowed & (coin | forced[:, None])
    starts = (slots == 0) | (slots == drawn[:, None]) | cuts
    segments = jnp.cumsum(starts.astype(jnp.int32), axis=1) - 1
    return (drawn, segments.reshape(-1).astype(jnp.int32))


def draw_counts(key, part):
    return layout(key)[0]


def draw_seg_ids(key, part):
    return layout(key)[1]


def draw_head_p(key, part):
    unit = jax.random.uniform(jax.random.fold_in(key, 17), (3, HEADS), jnp.float32)
    lower = jnp.array([-6.0, 0.0, 0.5], jnp.float32)[:, None]
    upper = jnp.array([-3.0, 2.5, 1.5], jnp.float32)[:, None]
    return (lower + (upper - lower) * unit).astype(jnp.float32)


def moment_draw(key, shape):
    first_key, second_key = jax.random.split(jax.random.fold_in(key, 11))
    spread = 0.03 * math.sqrt(TOKENS)
    first = spread * jnp.clip(jax.random.normal(first_key, shape, jnp.float32), -5.0, 5.0)
    second = TOKENS * jnp.exp(jax.random.uniform(second_key, shape, jnp.float32, math.log(1e-06), math.log(0.0001)))
    return jnp.stack([first, second]).astype(jnp.float32)


def draw_mom_in(key, part):
    return moment_draw(key, (D, PROJ))


def draw_mom_out(key, part):
    return moment_draw(key, (INNER, D))


def draw_mom_conv(key, part):
    return moment_draw(key, (KERNEL + 1, CONVD))


def draw_mom_norm(key, part):
    return moment_draw(key, (D,))


def draw_mom_gate(key, part):
    return moment_draw(key, (INNER,))


def draw_mom_head(key, part):
    return moment_draw(key, (3, HEADS))


def steps_of(own_key, shape, shards, smallest, high):
    factor_of, own = 1.0, jax.random.fold_in(own_key, 6)
    for position, blocks in shards:
        heights = jnp.exp(jax.random.uniform(jax.random.fold_in(own, position), (blocks,), jnp.float32, smallest / len(shards), high / len(shards)))
        factor_of = factor_of * jnp.repeat(heights, shape[position] // blocks).reshape([-1 if axis == position else 1 for axis in range(len(shape))])
    return factor_of


def bell_draw(rng, shape, width, bound, cuts=(), kind=jnp.bfloat16):
    values = jax.random.normal(rng, shape, jnp.float32) * width
    if len(cuts) > 0:
        values = steps_of(rng, shape, cuts, -0.22, 0.18) * values
    return jnp.clip(values, min=-bound, max=bound).astype(kind)


def setup_inputs(seed: int = 0) -> dict:
    splits = jax.random.split(jax.random.key(seed), 17)
    return {
        "x_in": bell_draw(splits[0], (TOKENS, D), 1.0, 6.0, ((0, 32),)),
        "cotangent": bell_draw(splits[1], (TOKENS, D), 1.0, 6.0, ((0, 32),)),
        "counts": draw_counts(jax.random.fold_in(splits[16], 71), 0),
        "seg_ids": draw_seg_ids(jax.random.fold_in(splits[16], 71), 0),
        "w_in": bell_draw(splits[4], (D, PROJ), D ** -0.5, 0.21875, ((0, 8),), jnp.float32),
        "w_out": bell_draw(splits[5], (INNER, D), INNER ** -0.5, 0.15625, ((0, 8),), jnp.float32),
        "conv_p": bell_draw(splits[6], (KERNEL + 1, CONVD), KERNEL ** -0.5, 3.0, ((1, 8),), jnp.float32),
        "norm_gain": jnp.clip(1.0 + 0.1 * jax.random.normal(splits[7], (D,), jnp.float32), 0.5, 1.5),
        "gate_gain": jnp.clip(1.0 + 0.1 * jax.random.normal(splits[8], (INNER,), jnp.float32), 0.5, 1.5),
        "head_p": draw_head_p(jax.random.fold_in(splits[16], 71), 0),
        "mom_in": draw_mom_in(jax.random.fold_in(splits[16], 71), 0),
        "mom_out": draw_mom_out(jax.random.fold_in(splits[16], 71), 0),
        "mom_conv": draw_mom_conv(jax.random.fold_in(splits[16], 71), 0),
        "mom_norm": draw_mom_norm(jax.random.fold_in(splits[16], 71), 0),
        "mom_gate": draw_mom_gate(jax.random.fold_in(splits[16], 71), 0),
        "mom_head": draw_mom_head(jax.random.fold_in(splits[16], 71), 0),
    }


norm_eps = 1e-05
adam_eps = 1e-08
beta_one = 0.9
beta_two = 0.999
rate_matrix = 0.01
rate_vector = 0.05
weight_decay = 0.1
highest = lax.Precision.HIGHEST

def mixer(proj, conv_taps, gate_w, head_params, seg_rows):
    length = proj.shape[0]
    nchunk = length // SPAN
    gate_z = proj[:, :INNER]
    conv_in = proj[:, INNER:INNER + CONVD]
    dt_raw = proj[:, INNER + CONVD:]
    summed = conv_taps[KERNEL] + conv_taps[KERNEL - 1] * conv_in
    for shift_by in range(1, KERNEL):
        earlier = jnp.concatenate([jnp.zeros((shift_by, CONVD), jnp.float32), conv_in[:length - shift_by]], axis=0)
        same_seg = jnp.concatenate([jnp.zeros((shift_by,), jnp.int32) == 1, seg_rows[shift_by:] == seg_rows[:length - shift_by]])
        summed = summed + conv_taps[KERNEL - 1 - shift_by] * jnp.where(same_seg[:, None], earlier, 0.0)
    conv_out = jax.nn.silu(summed)
    values = conv_out[:, :INNER].reshape(nchunk, SPAN, HEADS, HEADDIM)
    in_state = conv_out[:, INNER:INNER + STATE].reshape(nchunk, SPAN, STATE)
    out_state = conv_out[:, INNER + STATE:].reshape(nchunk, SPAN, STATE)
    step_size = jax.nn.softplus(dt_raw + head_params[0]).reshape(nchunk, SPAN, HEADS)
    log_decay = -step_size * jnp.exp(head_params[1])
    cumulative = jnp.cumsum(log_decay, axis=1)
    span_segs = seg_rows.reshape(nchunk, SPAN)
    rows_pos = jnp.arange(SPAN)
    causal = (rows_pos[:, None] >= rows_pos[None, :])[None] & (span_segs[:, :, None] == span_segs[:, None, :])
    cumul_heads = jnp.transpose(cumulative, (0, 2, 1))
    live_pairs = causal[:, None]
    contact = jnp.einsum('cqn,csn->cqs', out_state, in_state, precision=highest)
    step_heads = jnp.transpose(step_size, (0, 2, 1))
    spread = jnp.where(live_pairs, cumul_heads[:, :, :, None] - cumul_heads[:, :, None, :], 0.0)
    weights_qs = jnp.where(live_pairs, jnp.exp(spread) * contact[:, None] * step_heads[:, :, None, :], 0.0)
    inner_out = jnp.einsum('chqs,cshp->cqhp', weights_qs, values, precision=highest)
    last_seg = span_segs[:, SPAN - 1]
    keep_rows = span_segs == last_seg[:, None]
    tail_weight = jnp.exp(cumulative[:, SPAN - 1:, :] - cumulative) * step_size * keep_rows[:, :, None]
    span_state = jnp.einsum('csn,cshp->chnp', in_state, values * tail_weight[..., None], precision=highest)
    carry_state = span_state[0]
    carried = [jnp.zeros_like(values[0])]
    for span_no in range(1, nchunk):
        joined = span_segs[span_no] == last_seg[span_no - 1]
        entry_decay = jnp.exp(cumulative[span_no]) * joined[:, None]
        carried.append(jnp.einsum('qn,hnp->qhp', out_state[span_no], carry_state, precision=highest) * entry_decay[:, :, None])
        go_on = last_seg[span_no] == last_seg[span_no - 1]
        carry_state = jnp.where(go_on, jnp.exp(cumulative[span_no, SPAN - 1])[:, None, None] * carry_state, 0.0) + span_state[span_no]
    mixer_out = inner_out + jnp.stack(carried) + head_params[2][None, None, :, None] * values
    mixer_out = mixer_out.reshape(length, INNER)
    gated_out = mixer_out * jax.nn.silu(gate_z)
    row_scale = lax.rsqrt(lax.optimization_barrier(jnp.mean(gated_out * gated_out, axis=-1, keepdims=True)) + norm_eps)
    return gated_out * row_scale * gate_w

def adamw(weight, states, grad, rate, decay):
    first = beta_one * states[0] + (1.0 - beta_one) * grad
    second = beta_two * states[1] + (1.0 - beta_two) * grad * grad
    first_hat = first / (1.0 - beta_one ** STEP)
    second_hat = second / (1.0 - beta_two ** STEP)
    update = first_hat / (jnp.sqrt(second_hat) + adam_eps)
    return (weight - rate * (update + decay * weight), jnp.stack([first, second]))

def contract_rows(left, right):
    return lax.dot_general(left, right, (((0,), (0,)), ((), ())), preferred_element_type=jnp.float32)

def contract_cols(left, right):
    return lax.dot_general(left, right, (((1,), (1,)), ((), ())), preferred_element_type=jnp.float32)

def reference(x_in, cotangent, counts, seg_ids, w_in, w_out, conv_p, norm_gain, gate_gain, head_p, mom_in, mom_out, mom_conv, mom_norm, mom_gate, mom_head):
    full_in = w_in.astype(jnp.bfloat16)
    full_out = w_out.astype(jnp.bfloat16)
    conv_f = lax.optimization_barrier(conv_p.astype(jnp.bfloat16)).astype(jnp.float32)
    norm_f = lax.optimization_barrier(norm_gain.astype(jnp.bfloat16)).astype(jnp.float32)
    gate_f = lax.optimization_barrier(gate_gain.astype(jnp.bfloat16)).astype(jnp.float32)

    def block_step(totals, block):
        x_rows, cot_rows, count, seg_rows = block
        x_f = x_rows.astype(jnp.float32)
        inv_rms = lax.rsqrt(lax.optimization_barrier(jnp.mean(x_f * x_f, axis=-1, keepdims=True)) + norm_eps)
        normed = (x_f * inv_rms * norm_f).astype(jnp.bfloat16)
        proj = jnp.dot(normed, full_in, preferred_element_type=jnp.float32)

        def local_mixer(proj_in, conv_in, gate_in, head_in):
            return mixer(proj_in, conv_in, gate_in, head_in, seg_rows)
        mixer_f, mixer_back = jax.vjp(local_mixer, proj, conv_f, gate_f, head_p)
        mixer_b = mixer_f.astype(jnp.bfloat16)
        branch = jnp.dot(mixer_b, full_out, preferred_element_type=jnp.float32)
        live_rows = (jnp.arange(TOK_DEV) < count).astype(jnp.float32)[:, None]
        out_rows = (x_f + live_rows * branch).astype(jnp.bfloat16)
        cot_f = cot_rows.astype(jnp.float32)
        grad_branch = (live_rows * cot_f).astype(jnp.bfloat16)
        grad_w_out = contract_rows(mixer_b, grad_branch)
        grad_mixer = contract_cols(grad_branch, full_out)
        grad_proj, grad_conv, grad_gate, grad_head = mixer_back(grad_mixer)
        grad_proj_b = grad_proj.astype(jnp.bfloat16)
        grad_w_in = contract_rows(normed, grad_proj_b)
        grad_normed = contract_cols(grad_proj_b, full_in)
        grad_norm = lax.optimization_barrier(jnp.sum(grad_normed * x_f * inv_rms, axis=0))
        grad_hat = grad_normed * norm_f
        cube = inv_rms * inv_rms * inv_rms
        grad_x = cot_f + inv_rms * grad_hat - x_f * cube * lax.optimization_barrier(jnp.mean(x_f * grad_hat, axis=-1, keepdims=True))
        terms = (grad_w_in, grad_w_out, grad_conv, grad_norm, grad_gate, grad_head)
        return (tuple((a + b for a, b in zip(totals, terms))), (out_rows, grad_x))
    init = (jnp.zeros((D, PROJ), jnp.float32), jnp.zeros((INNER, D), jnp.float32), jnp.zeros((KERNEL + 1, CONVD), jnp.float32), jnp.zeros((D,), jnp.float32), jnp.zeros((INNER,), jnp.float32), jnp.zeros((3, HEADS), jnp.float32))
    blocks = (x_in.reshape(DEVICES, TOK_DEV, D), cotangent.reshape(DEVICES, TOK_DEV, D), counts, seg_ids.reshape(DEVICES, TOK_DEV))
    totals, (out_rows, grad_rows) = lax.scan(block_step, init, blocks)
    grad_in, grad_out, grad_conv, grad_norm, grad_gate, grad_head = totals
    new_in, new_mom_in = adamw(w_in, mom_in, grad_in, rate_matrix, weight_decay)
    new_out, new_mom_out = adamw(w_out, mom_out, grad_out, rate_matrix, weight_decay)
    new_conv, new_mom_conv = adamw(conv_p, mom_conv, grad_conv, rate_vector, 0.0)
    new_norm, new_mom_norm = adamw(norm_gain, mom_norm, grad_norm, rate_vector, 0.0)
    new_gate, new_mom_gate = adamw(gate_gain, mom_gate, grad_gate, rate_vector, 0.0)
    new_head, new_mom_head = adamw(head_p, mom_head, grad_head, rate_vector, 0.0)
    return (out_rows.reshape(TOKENS, D), grad_rows.reshape(TOKENS, D), grad_in, grad_out, grad_conv, grad_norm, grad_gate, grad_head, new_in, new_out, new_conv, new_norm, new_gate, new_head, new_mom_in, new_mom_out, new_mom_conv, new_mom_norm, new_mom_gate, new_mom_head)
```

```python
import functools

import jax
import jax.numpy as jnp
from jax import lax
from jax.sharding import PartitionSpec as P

HEADDIM = 64
STATE = 128
KERNEL = 4
SPAN = 256
STEP = 3
INNER = 1536
HEADS = 24
CONVD = 1792


norm_eps = 1e-05
adam_eps = 1e-08
beta_one = 0.9
beta_two = 0.999
rate_matrix = 0.01
rate_vector = 0.05
weight_decay = 0.1
precise = lax.Precision.HIGH


def mixer(gate_z, rest, conv_taps, gate_w, head_params, seg_rows):
    length = rest.shape[0]
    nchunk = length // SPAN
    conv_in = rest[:, :CONVD]
    dt_raw = rest[:, CONVD:]
    summed = conv_taps[KERNEL] + conv_taps[KERNEL - 1] * conv_in
    for shift_by in range(1, KERNEL):
        earlier = jnp.concatenate(
            [jnp.zeros((shift_by, CONVD), jnp.float32), conv_in[: length - shift_by]], axis=0
        )
        same_seg = jnp.concatenate(
            [
                jnp.zeros((shift_by,), jnp.int32) == 1,
                seg_rows[shift_by:] == seg_rows[: length - shift_by],
            ]
        )
        summed = summed + conv_taps[KERNEL - 1 - shift_by] * jnp.where(
            same_seg[:, None], earlier, 0.0
        )
    conv_out = jax.nn.silu(summed)
    values = conv_out[:, :INNER].reshape(nchunk, SPAN, HEADS, HEADDIM)
    in_state = conv_out[:, INNER : INNER + STATE].reshape(nchunk, SPAN, STATE)
    out_state = conv_out[:, INNER + STATE :].reshape(nchunk, SPAN, STATE)
    step_size = jax.nn.softplus(dt_raw + head_params[0]).reshape(nchunk, SPAN, HEADS)
    log_decay = -step_size * jnp.exp(head_params[1])
    cumulative = jnp.cumsum(log_decay, axis=1)
    span_segs = seg_rows.reshape(nchunk, SPAN)
    rows_pos = jnp.arange(SPAN)
    causal = (rows_pos[:, None] >= rows_pos[None, :])[None] & (
        span_segs[:, :, None] == span_segs[:, None, :]
    )
    cumul_heads = jnp.transpose(cumulative, (0, 2, 1))
    live_pairs = causal[:, None]
    contact = jnp.einsum("cqn,csn->cqs", out_state, in_state, precision=precise)
    step_heads = jnp.transpose(step_size, (0, 2, 1))
    spread = jnp.where(live_pairs, cumul_heads[:, :, :, None] - cumul_heads[:, :, None, :], 0.0)
    weights_qs = jnp.where(
        live_pairs, jnp.exp(spread) * contact[:, None] * step_heads[:, :, None, :], 0.0
    )
    inner_out = jnp.einsum("chqs,cshp->cqhp", weights_qs, values, precision=precise)
    mixer_out = inner_out + head_params[2][None, None, :, None] * values
    mixer_out = mixer_out.reshape(length, INNER)
    gated_out = mixer_out * jax.nn.silu(gate_z)
    row_scale = lax.rsqrt(jnp.mean(gated_out * gated_out, axis=-1, keepdims=True) + norm_eps)
    return gated_out * row_scale * gate_w


def adamw(weight, states, grad, rate, decay):
    first = beta_one * states[0] + (1.0 - beta_one) * grad
    second = beta_two * states[1] + (1.0 - beta_two) * grad * grad
    first_hat = first / (1.0 - beta_one**STEP)
    second_hat = second / (1.0 - beta_two**STEP)
    update = first_hat / (jnp.sqrt(second_hat) + adam_eps)
    return (weight - rate * (update + decay * weight), jnp.stack([first, second]))


def contract_rows(left, right):
    return lax.dot_general(
        left, right, (((0,), (0,)), ((), ())), preferred_element_type=jnp.float32
    )


def contract_cols(left, right):
    return lax.dot_general(
        left, right, (((1,), (1,)), ((), ())), preferred_element_type=jnp.float32
    )


def bits_of(count):
    return max(count.bit_length() - 1, 0)


def my_bit(sizes, axis):
    reps, shards_n = sizes
    low = bits_of(shards_n)
    if axis < low:
        return (lax.axis_index("shard") >> (low - 1 - axis)) & 1
    return (lax.axis_index("rep") >> (low + bits_of(reps) - 1 - axis)) & 1


def swap(sizes, axis, value):
    reps, shards_n = sizes
    low = bits_of(shards_n)
    high = low + bits_of(reps)
    mask = 1 << (low - 1 - axis) if axis < low else shards_n << (high - 1 - axis)
    pairs = [(i, i ^ mask) for i in range(reps * shards_n)]
    return lax.ppermute(value, ("rep", "shard"), pairs)


def gather_bits(sizes, piece, order):
    for axis in order:
        other = swap(sizes, axis, piece)
        first = my_bit(sizes, axis) == 0
        piece = jnp.concatenate(
            [jnp.where(first, piece, other), jnp.where(first, other, piece)], axis=axis
        )
    return piece


def scatter_bits(sizes, whole, order):
    for step, axis in enumerate(order):
        bit = my_bit(sizes, axis)
        sent = lax.dynamic_slice_in_dim(whole, 1 - bit, 1, axis)
        kept = lax.dynamic_slice_in_dim(whole, bit, 1, axis)
        came = swap(sizes, axis, sent)
        whole = kept.astype(jnp.float32) + came.astype(jnp.float32)
        if step < len(order) - 1:
            whole = whole.astype(jnp.bfloat16)
    return whole


def sum_bits(sizes, value, order):
    for axis in order:
        value = value + swap(sizes, axis, value)
    return value


def orders(sizes):
    reps, shards_n = sizes
    low, high = bits_of(shards_n), bits_of(shards_n) + bits_of(reps)
    ways_y = low // 2
    z_bits = list(range(low - ways_y))
    y_bits = list(range(low - ways_y, low))
    x_bits = list(range(low, high - 1))
    core_bits = list(range(high - 1, high))
    return z_bits, y_bits, x_bits, core_bits


def whole_weight(sizes, block, order):
    reps, shards_n = sizes
    bits = bits_of(reps) + bits_of(shards_n)
    rows = block.shape[0] // reps
    piece = lax.dynamic_slice_in_dim(block, lax.axis_index("rep") * rows, rows, 0)
    piece = piece.astype(jnp.bfloat16).reshape((1,) * bits + (rows, block.shape[1]))
    return gather_bits(sizes, piece, order).reshape(block.shape[0] * shards_n, block.shape[1])


def owned_sum(sizes, grad, order):
    reps, shards_n = sizes
    bits = bits_of(reps) + bits_of(shards_n)
    low = bits_of(shards_n)
    rows = grad.shape[0] // (reps * shards_n)
    pieces = grad.astype(jnp.bfloat16).reshape((2,) * bits + (rows, grad.shape[1]))
    own = scatter_bits(sizes, pieces, order).astype(jnp.bfloat16)
    own = gather_bits(sizes, own, list(range(low, bits)))
    return own.reshape(rows * reps, grad.shape[1]).astype(jnp.float32)


def shards(
    sizes,
    x_in,
    cotangent,
    counts,
    seg_ids,
    w_in,
    w_out,
    conv_p,
    norm_gain,
    gate_gain,
    head_p,
    mom_in,
    mom_out,
    mom_conv,
    mom_norm,
    mom_gate,
    mom_head,
):
    low = jnp.bfloat16
    z_bits, y_bits, x_bits, core_bits = orders(sizes)
    reps, shards_n = sizes
    me = lax.axis_index("shard")
    parts = (conv_p.reshape(1, -1), norm_gain[None], gate_gain[None])
    small = jnp.concatenate([part.astype(low) for part in parts], axis=1)
    shard_bits = bits_of(shards_n)
    small = small.reshape((1,) * shard_bits + small.shape)
    small = gather_bits(sizes, small, list(range(shard_bits))).reshape(shards_n, -1)
    taps, conv_cols = conv_p.shape
    gain_cols = norm_gain.shape[0]
    conv_f = small[:, : taps * conv_cols].reshape(shards_n, taps, conv_cols)
    conv_f = jnp.transpose(conv_f, (1, 0, 2)).reshape(taps, -1).astype(jnp.float32)
    norm_f = small[:, taps * conv_cols : taps * conv_cols + gain_cols].reshape(-1)
    norm_f = norm_f.astype(jnp.float32)
    gate_f = small[:, taps * conv_cols + gain_cols :].reshape(-1).astype(jnp.float32)
    far_first = z_bits + y_bits + x_bits + core_bits
    side_first = z_bits + x_bits + y_bits + core_bits
    full_rest = whole_weight(sizes, w_in[:, INNER:], far_first)
    full_z = whole_weight(sizes, w_in[:, :INNER], side_first)
    full_out = whole_weight(sizes, w_out, far_first)
    x_f = x_in.astype(jnp.float32)
    inv_rms = lax.rsqrt(jnp.mean(x_f * x_f, axis=-1, keepdims=True) + norm_eps)
    normed = (x_f * inv_rms * norm_f).astype(low)
    rest = jnp.dot(normed, full_rest, preferred_element_type=jnp.float32)
    gate_z = jnp.dot(normed, full_z, preferred_element_type=jnp.float32)

    def local_mixer(z_in, rest_in, conv_in, gate_in, head_in):
        return mixer(z_in, rest_in, conv_in, gate_in, head_in, seg_ids)

    mixer_f, mixer_back = jax.vjp(local_mixer, gate_z, rest, conv_f, gate_f, head_p)
    mixer_b = mixer_f.astype(low)
    branch = jnp.dot(mixer_b, full_out, preferred_element_type=jnp.float32)
    live_rows = (jnp.arange(x_in.shape[0]) < counts[0]).astype(jnp.float32)[:, None]
    block_out = (x_f + live_rows * branch).astype(low)
    cot_f = cotangent.astype(jnp.float32)
    grad_branch = (live_rows * cot_f).astype(low)
    near_last = core_bits + x_bits + y_bits + z_bits[::-1]
    side_last = core_bits + y_bits + x_bits + z_bits[::-1]
    own_out = owned_sum(sizes, contract_rows(mixer_b, grad_branch), side_last)
    grad_mixer = contract_cols(grad_branch, full_out)
    grad_z, grad_rest, grad_conv, grad_gate, grad_head = mixer_back(grad_mixer)
    grad_z_b = grad_z.astype(low)
    grad_rest_b = grad_rest.astype(low)
    own_z = owned_sum(sizes, contract_rows(normed, grad_z_b), side_last)
    own_rest = owned_sum(sizes, contract_rows(normed, grad_rest_b), near_last)
    grad_normed = contract_cols(grad_z_b, full_z) + contract_cols(grad_rest_b, full_rest)
    grad_norm = jnp.sum(grad_normed * x_f * inv_rms, axis=0)
    grad_hat = grad_normed * norm_f
    cube = inv_rms * inv_rms * inv_rms
    input_grad = (
        cot_f + inv_rms * grad_hat - x_f * cube * jnp.mean(x_f * grad_hat, axis=-1, keepdims=True)
    )
    flat = jnp.concatenate(
        [grad_conv.reshape(-1), grad_norm, grad_gate, grad_head.reshape(-1)]
    )
    flat = jnp.pad(flat, (0, -flat.shape[0] % 1024)).reshape(-1, 128)
    total = sum_bits(sizes, flat, near_last).reshape(-1)
    sums, start = [], 0
    for like in (grad_conv, grad_norm, grad_gate, grad_head):
        sums.append(total[start : start + like.size].reshape(like.shape))
        start += like.size
    own_conv = lax.dynamic_slice_in_dim(sums[0], me * conv_cols, conv_cols, 1)
    own_norm = lax.dynamic_slice_in_dim(sums[1], me * gain_cols, gain_cols, 0)
    own_gate = lax.dynamic_slice_in_dim(
        sums[2], me * gate_gain.shape[0], gate_gain.shape[0], 0
    )
    head_total = sums[3]
    own_in = jnp.concatenate([own_z, own_rest], axis=1)
    new_in, new_mom_in = adamw(w_in, mom_in, own_in, rate_matrix, weight_decay)
    new_out, new_mom_out = adamw(w_out, mom_out, own_out, rate_matrix, weight_decay)
    new_conv, new_mom_conv = adamw(conv_p, mom_conv, own_conv, rate_vector, 0.0)
    new_norm, new_mom_norm = adamw(norm_gain, mom_norm, own_norm, rate_vector, 0.0)
    new_gate, new_mom_gate = adamw(gate_gain, mom_gate, own_gate, rate_vector, 0.0)
    new_head, new_mom_head = adamw(head_p, mom_head, head_total, rate_vector, 0.0)
    return (
        block_out,
        input_grad,
        own_in,
        own_out,
        own_conv,
        own_norm,
        own_gate,
        head_total,
        new_in,
        new_out,
        new_conv,
        new_norm,
        new_gate,
        new_head,
        new_mom_in,
        new_mom_out,
        new_mom_conv,
        new_mom_norm,
        new_mom_gate,
        new_mom_head,
    )


def solution(mesh):
    sizes = (mesh.shape["rep"], mesh.shape["shard"])
    return jax.shard_map(
        functools.partial(shards, sizes),
        mesh=mesh,
        in_specs=(
            P(("rep", "shard"), None),
            P(("rep", "shard"), None),
            P(("rep", "shard")),
            P(("rep", "shard")),
            P("shard", None),
            P("shard", None),
            P(None, "shard"),
            P("shard"),
            P("shard"),
            P(),
            P(None, "shard", None),
            P(None, "shard", None),
            P(None, None, "shard"),
            P(None, "shard"),
            P(None, "shard"),
            P(),
        ),
        out_specs=(
            P(("rep", "shard"), None),
            P(("rep", "shard"), None),
            P("shard", None),
            P("shard", None),
            P(None, "shard"),
            P("shard"),
            P("shard"),
            P(),
            P("shard", None),
            P("shard", None),
            P(None, "shard"),
            P("shard"),
            P("shard"),
            P(),
            P(None, "shard", None),
            P(None, "shard", None),
            P(None, None, "shard"),
            P(None, "shard"),
            P(None, "shard"),
            P(),
        ),
        check_vma=False,
    )
```

```python
import functools

import jax
import jax.numpy as jnp
from jax import lax
from jax.sharding import PartitionSpec as P

HEADDIM = 64
STATE = 128
KERNEL = 4
SPAN = 256
STEP = 3
INNER = 1536
HEADS = 24
CONVD = 1792


norm_eps = 1e-05
adam_eps = 1e-08
beta_one = 0.9
beta_two = 0.999
rate_matrix = 0.01
rate_vector = 0.05
weight_decay = 0.1
precise = lax.Precision.HIGH


def mixer(gate_z, rest, conv_taps, gate_w, head_params, seg_rows):
    length = rest.shape[0]
    nchunk = length // SPAN
    conv_in = rest[:, :CONVD]
    dt_raw = rest[:, CONVD:]
    summed = conv_taps[KERNEL] + conv_taps[KERNEL - 1] * conv_in
    for shift_by in range(1, KERNEL):
        earlier = jnp.concatenate(
            [jnp.zeros((shift_by, CONVD), jnp.float32), conv_in[: length - shift_by]], axis=0
        )
        same_seg = jnp.concatenate(
            [
                jnp.zeros((shift_by,), jnp.int32) == 1,
                seg_rows[shift_by:] == seg_rows[: length - shift_by],
            ]
        )
        summed = summed + conv_taps[KERNEL - 1 - shift_by] * jnp.where(
            same_seg[:, None], earlier, 0.0
        )
    conv_out = jax.nn.silu(summed)
    values = conv_out[:, :INNER].reshape(nchunk, SPAN, HEADS, HEADDIM)
    in_state = conv_out[:, INNER : INNER + STATE].reshape(nchunk, SPAN, STATE)
    out_state = conv_out[:, INNER + STATE :].reshape(nchunk, SPAN, STATE)
    step_size = jax.nn.softplus(dt_raw + head_params[0]).reshape(nchunk, SPAN, HEADS)
    log_decay = -step_size * jnp.exp(head_params[1])
    cumulative = jnp.cumsum(log_decay, axis=1)
    span_segs = seg_rows.reshape(nchunk, SPAN)
    rows_pos = jnp.arange(SPAN)
    causal = (rows_pos[:, None] >= rows_pos[None, :])[None] & (
        span_segs[:, :, None] == span_segs[:, None, :]
    )
    cumul_heads = jnp.transpose(cumulative, (0, 2, 1))
    live_pairs = causal[:, None]
    contact = jnp.einsum("cqn,csn->cqs", out_state, in_state, precision=precise)
    step_heads = jnp.transpose(step_size, (0, 2, 1))
    spread = jnp.where(live_pairs, cumul_heads[:, :, :, None] - cumul_heads[:, :, None, :], 0.0)
    weights_qs = jnp.where(
        live_pairs, jnp.exp(spread) * contact[:, None] * step_heads[:, :, None, :], 0.0
    )
    inner_out = jnp.einsum("chqs,cshp->cqhp", weights_qs, values, precision=precise)
    mixer_out = inner_out + head_params[2][None, None, :, None] * values
    mixer_out = mixer_out.reshape(length, INNER)
    gated_out = mixer_out * jax.nn.silu(gate_z)
    row_scale = lax.rsqrt(jnp.mean(gated_out * gated_out, axis=-1, keepdims=True) + norm_eps)
    return gated_out * row_scale * gate_w


def adamw(weight, states, grad, rate, decay):
    first = beta_one * states[0] + (1.0 - beta_one) * grad
    second = beta_two * states[1] + (1.0 - beta_two) * grad * grad
    first_hat = first / (1.0 - beta_one**STEP)
    second_hat = second / (1.0 - beta_two**STEP)
    update = first_hat / (jnp.sqrt(second_hat) + adam_eps)
    return (weight - rate * (update + decay * weight), jnp.stack([first, second]))


def contract_rows(left, right):
    return lax.dot_general(
        left, right, (((0,), (0,)), ((), ())), preferred_element_type=jnp.float32
    )


def contract_cols(left, right):
    return lax.dot_general(
        left, right, (((1,), (1,)), ((), ())), preferred_element_type=jnp.float32
    )


def bits_of(count):
    return max(count.bit_length() - 1, 0)


def my_bit(sizes, axis):
    reps, shards_n = sizes
    low = bits_of(shards_n)
    if axis < low:
        return (lax.axis_index("shard") >> (low - 1 - axis)) & 1
    return (lax.axis_index("rep") >> (low + bits_of(reps) - 1 - axis)) & 1


def swap(sizes, axis, value):
    reps, shards_n = sizes
    low = bits_of(shards_n)
    high = low + bits_of(reps)
    mask = 1 << (low - 1 - axis) if axis < low else shards_n << (high - 1 - axis)
    pairs = [(i, i ^ mask) for i in range(reps * shards_n)]
    return lax.ppermute(value, ("rep", "shard"), pairs)


def gather_bits(sizes, piece, order):
    for axis in order:
        other = swap(sizes, axis, piece)
        first = my_bit(sizes, axis) == 0
        piece = jnp.concatenate(
            [jnp.where(first, piece, other), jnp.where(first, other, piece)], axis=axis
        )
    return piece


def scatter_bits(sizes, whole, order):
    for step, axis in enumerate(order):
        bit = my_bit(sizes, axis)
        sent = lax.dynamic_slice_in_dim(whole, 1 - bit, 1, axis)
        kept = lax.dynamic_slice_in_dim(whole, bit, 1, axis)
        came = swap(sizes, axis, sent)
        whole = kept.astype(jnp.float32) + came.astype(jnp.float32)
        if step < len(order) - 1:
            whole = whole.astype(jnp.bfloat16)
    return whole


def sum_bits(sizes, value, order):
    for axis in order:
        value = value + swap(sizes, axis, value)
    return value


def orders(sizes):
    reps, shards_n = sizes
    low, high = bits_of(shards_n), bits_of(shards_n) + bits_of(reps)
    ways_y = low // 2
    z_bits = list(range(low - ways_y))
    y_bits = list(range(low - ways_y, low))
    x_bits = list(range(low, high - 1))
    core_bits = list(range(high - 1, high))
    return z_bits, y_bits, x_bits, core_bits


def own_piece(sizes, block):
    reps, shards_n = sizes
    bits = bits_of(reps) + bits_of(shards_n)
    rows = block.shape[0] // reps
    piece = lax.dynamic_slice_in_dim(block, lax.axis_index("rep") * rows, rows, 0)
    return piece.astype(jnp.bfloat16).reshape((1,) * bits + (rows, block.shape[1]))


def as_rows(pieces):
    return pieces.reshape(-1, pieces.shape[-1])


def as_pieces(sizes, grad):
    reps, shards_n = sizes
    bits = bits_of(reps) + bits_of(shards_n)
    rows = grad.shape[0] // (reps * shards_n)
    return grad.astype(jnp.bfloat16).reshape((2,) * bits + (rows, grad.shape[1]))


def shared_over_rep(sizes, own):
    reps, shards_n = sizes
    low = bits_of(shards_n)
    own = gather_bits(sizes, own.astype(jnp.bfloat16), list(range(low, low + bits_of(reps))))
    return as_rows(own).astype(jnp.float32)


def shards(
    sizes,
    x_in,
    cotangent,
    counts,
    seg_ids,
    w_in,
    w_out,
    conv_p,
    norm_gain,
    gate_gain,
    head_p,
    mom_in,
    mom_out,
    mom_conv,
    mom_norm,
    mom_gate,
    mom_head,
):
    low = jnp.bfloat16
    z_bits, y_bits, x_bits, core_bits = orders(sizes)
    reps, shards_n = sizes
    me = lax.axis_index("shard")
    parts = (conv_p.reshape(1, -1), norm_gain[None], gate_gain[None])
    small = jnp.concatenate([part.astype(low) for part in parts], axis=1)
    shard_bits = bits_of(shards_n)
    small = small.reshape((1,) * shard_bits + small.shape)
    small = gather_bits(sizes, small, list(range(shard_bits))).reshape(shards_n, -1)
    taps, conv_cols = conv_p.shape
    gain_cols = norm_gain.shape[0]
    conv_f = small[:, : taps * conv_cols].reshape(shards_n, taps, conv_cols)
    conv_f = jnp.transpose(conv_f, (1, 0, 2)).reshape(taps, -1).astype(jnp.float32)
    norm_f = small[:, taps * conv_cols : taps * conv_cols + gain_cols].reshape(-1)
    norm_f = norm_f.astype(jnp.float32)
    gate_f = small[:, taps * conv_cols + gain_cols :].reshape(-1).astype(jnp.float32)
    piece_in = gather_bits(sizes, own_piece(sizes, w_in), z_bits)
    full_rest = as_rows(
        gather_bits(sizes, piece_in[..., INNER:], y_bits + x_bits + core_bits)
    )
    full_z = as_rows(gather_bits(sizes, piece_in[..., :INNER], x_bits + y_bits + core_bits))
    far_first = z_bits + y_bits + x_bits + core_bits
    full_out = as_rows(gather_bits(sizes, own_piece(sizes, w_out), far_first))
    x_f = x_in.astype(jnp.float32)
    inv_rms = lax.rsqrt(jnp.mean(x_f * x_f, axis=-1, keepdims=True) + norm_eps)
    normed = (x_f * inv_rms * norm_f).astype(low)
    rest = jnp.dot(normed, full_rest, preferred_element_type=jnp.float32)
    gate_z = jnp.dot(normed, full_z, preferred_element_type=jnp.float32)

    def local_mixer(z_in, rest_in, conv_in, gate_in, head_in):
        return mixer(z_in, rest_in, conv_in, gate_in, head_in, seg_ids)

    mixer_f, mixer_back = jax.vjp(local_mixer, gate_z, rest, conv_f, gate_f, head_p)
    mixer_b = mixer_f.astype(low)
    branch = jnp.dot(mixer_b, full_out, preferred_element_type=jnp.float32)
    live_rows = (jnp.arange(x_in.shape[0]) < counts[0]).astype(jnp.float32)[:, None]
    block_out = (x_f + live_rows * branch).astype(low)
    cot_f = cotangent.astype(jnp.float32)
    grad_branch = (live_rows * cot_f).astype(low)
    near_last = core_bits + x_bits + y_bits + z_bits[::-1]
    side_last = core_bits + y_bits + x_bits + z_bits[::-1]
    grad_out = as_pieces(sizes, contract_rows(mixer_b, grad_branch))
    own_out = shared_over_rep(sizes, scatter_bits(sizes, grad_out, side_last))
    grad_mixer = contract_cols(grad_branch, full_out)
    grad_z, grad_rest, grad_conv, grad_gate, grad_head = mixer_back(grad_mixer)
    grad_z_b = grad_z.astype(low)
    grad_rest_b = grad_rest.astype(low)
    grad_normed = contract_cols(grad_z_b, full_z) + contract_cols(grad_rest_b, full_rest)
    grad_norm = jnp.sum(grad_normed * x_f * inv_rms, axis=0)
    grad_hat = grad_normed * norm_f
    cube = inv_rms * inv_rms * inv_rms
    input_grad = (
        cot_f + inv_rms * grad_hat - x_f * cube * jnp.mean(x_f * grad_hat, axis=-1, keepdims=True)
    )
    flat = jnp.concatenate(
        [grad_conv.reshape(-1), grad_norm, grad_gate, grad_head.reshape(-1)]
    )
    flat = jnp.pad(flat, (0, -flat.shape[0] % 1024)).reshape(-1, 128)
    flat, grad_rest_b = lax.optimization_barrier((flat, grad_rest_b))
    pieces_z = as_pieces(sizes, contract_rows(normed, grad_z_b))
    pieces_z = scatter_bits(sizes, pieces_z, core_bits).astype(low)
    pieces_rest = as_pieces(sizes, contract_rows(normed, grad_rest_b))
    pieces_rest = scatter_bits(sizes, pieces_rest, core_bits).astype(low)
    flat, pieces_z, pieces_rest = lax.optimization_barrier((flat, pieces_z, pieces_rest))
    pieces_z = scatter_bits(sizes, pieces_z, y_bits + x_bits)
    pieces_rest = scatter_bits(sizes, pieces_rest, x_bits + y_bits)
    pieces_in = jnp.concatenate([pieces_z, pieces_rest], axis=-1).astype(low)
    own_in = shared_over_rep(sizes, scatter_bits(sizes, pieces_in, z_bits[::-1]))
    total = sum_bits(sizes, flat, near_last).reshape(-1)
    sums, start = [], 0
    for like in (grad_conv, grad_norm, grad_gate, grad_head):
        sums.append(total[start : start + like.size].reshape(like.shape))
        start += like.size
    own_conv = lax.dynamic_slice_in_dim(sums[0], me * conv_cols, conv_cols, 1)
    own_norm = lax.dynamic_slice_in_dim(sums[1], me * gain_cols, gain_cols, 0)
    own_gate = lax.dynamic_slice_in_dim(
        sums[2], me * gate_gain.shape[0], gate_gain.shape[0], 0
    )
    head_total = sums[3]
    new_in, new_mom_in = adamw(w_in, mom_in, own_in, rate_matrix, weight_decay)
    new_out, new_mom_out = adamw(w_out, mom_out, own_out, rate_matrix, weight_decay)
    new_conv, new_mom_conv = adamw(conv_p, mom_conv, own_conv, rate_vector, 0.0)
    new_norm, new_mom_norm = adamw(norm_gain, mom_norm, own_norm, rate_vector, 0.0)
    new_gate, new_mom_gate = adamw(gate_gain, mom_gate, own_gate, rate_vector, 0.0)
    new_head, new_mom_head = adamw(head_p, mom_head, head_total, rate_vector, 0.0)
    return (
        block_out,
        input_grad,
        own_in,
        own_out,
        own_conv,
        own_norm,
        own_gate,
        head_total,
        new_in,
        new_out,
        new_conv,
        new_norm,
        new_gate,
        new_head,
        new_mom_in,
        new_mom_out,
        new_mom_conv,
        new_mom_norm,
        new_mom_gate,
        new_mom_head,
    )


def solution(mesh):
    sizes = (mesh.shape["rep"], mesh.shape["shard"])
    return jax.shard_map(
        functools.partial(shards, sizes),
        mesh=mesh,
        in_specs=(
            P(("rep", "shard"), None),
            P(("rep", "shard"), None),
            P(("rep", "shard")),
            P(("rep", "shard")),
            P("shard", None),
            P("shard", None),
            P(None, "shard"),
            P("shard"),
            P("shard"),
            P(),
            P(None, "shard", None),
            P(None, "shard", None),
            P(None, None, "shard"),
            P(None, "shard"),
            P(None, "shard"),
            P(),
        ),
        out_specs=(
            P(("rep", "shard"), None),
            P(("rep", "shard"), None),
            P("shard", None),
            P("shard", None),
            P(None, "shard"),
            P("shard"),
            P("shard"),
            P(),
            P("shard", None),
            P("shard", None),
            P(None, "shard"),
            P("shard"),
            P("shard"),
            P(),
            P(None, "shard", None),
            P(None, "shard", None),
            P(None, None, "shard"),
            P(None, "shard"),
            P(None, "shard"),
            P(),
        ),
        check_vma=False,
    )
```
